512 devices in a mesh: blk: 64 (over y, z_lo, core), group: 8 (over x, z_hi).
Axes of the slice: x: 4, y: 4, z: 16 (z_hi: 2, z_lo: 8; z = z_hi * 8 + z_lo), core: 2. Of those that a mesh axis runs over, the one named last changes fastest.
Arguments:
- audio_embed: float32 [49152, 512], P('blk'), may hold values from -4 to 4
- text_embed: float32 [49152, 512], P(('blk', 'group')), may hold values from -4 to 4
Outputs:
- grad_audio: float32 [49152, 512], P(('blk', 'group'))
- grad_text: float32 [49152, 512], P(('blk', 'group'))
- loss_rows: float32 [49152], P(('blk', 'group'))
- loss_cols: float32 [49152], P(('blk', 'group'))
The draws below stay inside these ranges and needn't reach their ends.
All inputs are finite; a program needn't handle non-finite values.
Results may differ from the reference program's by a relative error of at most 0.0003.
Values sent between devices are 32-bit elements; how exact they have to be, the bound alone decides.
No kernel may reach another device: no remote copies, remote signals or barrier semaphores. Data moves between devices by JAX's collectives and lax.ppermute only.
A program may use at most 64 MiB of HBM per device.

```python
import jax
import jax.numpy as jnp
from jax import lax

D = 512
RB = 768
SPAN = 3
PAIRS = 49152
N_BLK = 64


def joint_draw(key):
    subkeys = jax.random.split(jax.random.fold_in(key, 11), 2)
    audio_noise = jax.random.normal(subkeys[0], (PAIRS, D), jnp.float32)
    text_noise = jax.random.normal(subkeys[1], (PAIRS, D), jnp.float32)
    audio_out = 0.1 * audio_noise
    text_out = 0.1 * text_noise
    return (jnp.clip(audio_out, -4.0, 4.0), jnp.clip(text_out, -4.0, 4.0))


def draw_audio_embed(key, part):
    return joint_draw(key)[0]


def draw_text_embed(key, part):
    return joint_draw(key)[1]


def setup_inputs(seed: int = 0) -> dict:
    seeds = jax.random.split(jax.random.key(seed), 3)
    return {
        "audio_embed": draw_audio_embed(jax.random.fold_in(seeds[2], 71), 0),
        "text_embed": draw_text_embed(jax.random.fold_in(seeds[2], 71), 0),
    }


logit_scale = 1.0 / 0.07
precise = lax.Precision.HIGHEST


def window_blocks(blocks, block):
    picked = ((block + jnp.arange(SPAN, dtype=jnp.int32)) % N_BLK).astype(jnp.int32)
    return jnp.take(blocks, picked, axis=0)


def scores(audio_block, window):
    return logit_scale * jnp.einsum("rd,kcd->rkc", audio_block, window, precision=precise)


def reference(audio_embed, text_embed):
    text_blocks = text_embed.reshape(N_BLK, RB, D)
    audio_blocks = audio_embed.reshape(N_BLK, RB, D)
    indices = jnp.arange(N_BLK, dtype=jnp.int32)

    def forward(block):
        audio_block = lax.dynamic_index_in_dim(audio_blocks, block, 0, keepdims=False)
        logits = scores(audio_block, window_blocks(text_blocks, block))
        row_top = jnp.max(logits, axis=(1, 2))
        row_lse = row_top + jnp.log(jnp.sum(jnp.exp(logits - row_top[:, None, None]), axis=(1, 2)))
        col_top = jnp.max(logits, axis=0)
        col_sum = jnp.sum(jnp.exp(logits - col_top[None]), axis=0)
        return row_lse, col_top, col_sum

    row_lse, col_top, col_sum = lax.map(forward, indices)
    tile_maxima = jnp.stack([jnp.roll(col_top[:, offset], offset, axis=0) for offset in range(SPAN)])
    tile_sums = jnp.stack([jnp.roll(col_sum[:, offset], offset, axis=0) for offset in range(SPAN)])
    highest = jnp.max(tile_maxima, axis=0)
    col_lse = highest + jnp.log(jnp.sum(tile_sums * jnp.exp(tile_maxima - highest[None]), axis=0))
    positive = jnp.eye(RB, dtype=jnp.float32)[:, None, :] * (jnp.arange(SPAN) == 0).astype(jnp.float32)[None, :, None]

    def backward(block):
        audio_block = lax.dynamic_index_in_dim(audio_blocks, block, 0, keepdims=False)
        window = window_blocks(text_blocks, block)
        logits = scores(audio_block, window)
        lse_window = window_blocks(col_lse, block)
        row_block = lax.dynamic_index_in_dim(row_lse, block, 0, keepdims=False)
        soft_weights = 0.5 * (jnp.exp(logits - row_block[:, None, None]) + jnp.exp(logits - lse_window[None]))
        grad_logits = soft_weights - positive
        audio_part = logit_scale * jnp.einsum("rkc,kcd->rd", grad_logits, window, precision=precise)
        text_parts = logit_scale * jnp.einsum("rkc,rd->kcd", grad_logits, audio_block, precision=precise)
        positive_scores = jnp.diagonal(logits[:, 0, :])
        return audio_part, text_parts, row_block - positive_scores, positive_scores

    audio_parts, text_parts, loss_rows, positive_scores = lax.map(backward, indices)
    grad_text = text_parts[:, 0]
    for offset in range(1, SPAN):
        grad_text = grad_text + jnp.roll(text_parts[:, offset], offset, axis=0)
    loss_cols = col_lse - positive_scores
    return (audio_parts.reshape(PAIRS, D), grad_text.reshape(PAIRS, D), loss_rows.reshape(PAIRS), loss_cols.reshape(PAIRS))
```

```python
import jax
import jax.numpy as jnp
from jax import lax
from jax.sharding import PartitionSpec as P

SPAN = 3
BLOCKS = 64
GROUP = 8

logit_scale = 1.0 / 0.07
precise = lax.Precision.HIGHEST
both = ("blk", "group")


def send(value, target):
    pairs = []
    for block in range(BLOCKS):
        for member in range(GROUP):
            to_block, to_member = target(block, member)
            pairs.append((block * GROUP + member, to_block * GROUP + to_member))
    return lax.ppermute(value, both, pairs)


def ring(by):
    def target(block, member):
        to_block = (block + by) % BLOCKS
        crossed = ((block >> 4) ^ (to_block >> 4)) & 1
        return to_block, member ^ crossed

    return target


def mate(block, member):
    return block ^ 1, member


def across(block, member):
    return block, member ^ 1


def flip_x(bits):
    return lambda block, member: (block, member ^ (bits << 1))


def turn_x(by):
    return lambda block, member: (block, (((member >> 1) + by) % 4) * 2 + (member & 1))


def merge(one, two):
    highest = jnp.maximum(one[0], two[0])
    return jnp.stack(
        [highest, one[1] * jnp.exp(one[0] - highest) + two[1] * jnp.exp(two[0] - highest)]
    )


def rolled(value, by):
    return lax.dynamic_slice_in_dim(jnp.concatenate([value, value], 0), by, 4, 0)


def shards(audio_embed, text_embed):
    rows, width = audio_embed.shape
    cols = text_embed.shape[0]
    block = lax.axis_index("blk")
    member = lax.axis_index("group")
    core = block % 2
    x, half = member // 2, member % 2

    two_on = send(text_embed, ring(-2))
    one_on = send(text_embed, ring(-1))
    other_text = send(text_embed, across)

    chunks = audio_embed.reshape(4, 2, cols, width)
    mine = jnp.where(half == 0, chunks[:, 0], chunks[:, 1])
    others = jnp.where(half == 0, chunks[:, 1], chunks[:, 0])
    audio_mine = rolled(mine, x).reshape(4 * cols, width)
    audio = jnp.concatenate([audio_mine, rolled(others, x).reshape(4 * cols, width)])

    def to_plain(value):
        own, other = rolled(value[0:4], (4 - x) % 4), rolled(value[4:8], (4 - x) % 4)
        return jnp.where(half == 0, jnp.stack([own, other], 1), jnp.stack([other, own], 1))

    def from_plain(value):
        own = jnp.where(half == 0, value[:, 0], value[:, 1])
        other = jnp.where(half == 0, value[:, 1], value[:, 0])
        return jnp.concatenate([rolled(own, x), rolled(other, x)])

    window = jnp.stack([text_embed, one_on, two_on])
    logits = logit_scale * jnp.einsum("rd,kcd->rkc", audio, window, precision=precise)
    row_top = jnp.max(logits, axis=(1, 2))
    row_sum = jnp.sum(jnp.exp(logits - row_top[:, None, None]), axis=(1, 2))
    col_top = jnp.max(logits, axis=0)
    col_sum = jnp.sum(jnp.exp(logits - col_top[None]), axis=0)

    row_stat = jnp.stack(
        [to_plain(row_top.reshape(8, cols)), to_plain(row_sum.reshape(8, cols))]
    ).reshape(2, rows)
    col_stat = jnp.stack([col_top, col_sum])
    row_one = send(row_stat, flip_x(1))
    before = send(col_stat, ring(2))
    after = send(col_stat, ring(-2))
    row_stat = merge(row_stat, row_one)
    row_stat = merge(row_stat, send(row_stat, flip_x(3)))
    beside = send(jnp.stack([col_stat, before, after]), mate)
    one_before = jnp.where(core == 0, beside[1], beside[0])
    one_after = jnp.where(core == 0, beside[0], beside[2])
    stat_0 = merge(merge(before[:, 2], one_before[:, 1]), col_stat[:, 0])
    stat_1 = merge(merge(one_before[:, 2], col_stat[:, 1]), one_after[:, 0])
    stat_2 = merge(merge(col_stat[:, 2], one_after[:, 1]), after[:, 0])
    col_stat = jnp.stack([stat_0, stat_1, stat_2], 1)
    col_lse = col_stat[0] + jnp.log(col_stat[1])

    passed = send(jnp.concatenate([row_stat.reshape(-1), col_lse.reshape(-1)]), across)
    other_rows = passed[: 2 * rows].reshape(2, rows)
    other_col_lse = passed[2 * rows :].reshape(SPAN, cols)
    row_stat = merge(row_stat, other_rows)
    row_lse_plain = row_stat[0] + jnp.log(row_stat[1])
    row_lse = from_plain(row_lse_plain.reshape(4, 2, cols)).reshape(rows)

    other_two = send(other_text, ring(-2))
    other_one = send(other_text, ring(-1))
    other_window = jnp.stack([other_text, other_one, other_two])
    other_logits = logit_scale * jnp.einsum(
        "rd,kcd->rkc", audio_mine, other_window, precision=precise
    )

    def weights(scores, by_row, by_col):
        return 0.5 * (
            jnp.exp(scores - by_row[:, None, None]) + jnp.exp(scores - by_col[None])
        )

    shape = (rows, SPAN, cols)
    positive = (lax.broadcasted_iota(jnp.int32, shape, 1) == 0) & (
        lax.broadcasted_iota(jnp.int32, shape, 0) == lax.broadcasted_iota(jnp.int32, shape, 2)
    )
    grad_logits = weights(logits, row_lse, col_lse) - positive.astype(jnp.float32)
    other_grad = weights(other_logits, row_lse[: 4 * cols], other_col_lse)

    text_parts = logit_scale * jnp.einsum("rkc,rd->kcd", grad_logits, audio, precision=precise)
    from_mate = send(text_parts[1], mate)
    ahead = text_parts[2] + jnp.where(core == 0, from_mate, 0.0)
    grad_text = text_parts[0] + jnp.where(core == 1, from_mate, 0.0) + send(ahead, ring(2))

    audio_parts = logit_scale * (
        jnp.einsum("rkc,kcd->rd", grad_logits[: 4 * cols], window, precision=precise)
        + jnp.einsum("rkc,kcd->rd", other_grad, other_window, precision=precise)
    )
    audio_parts = audio_parts.reshape(4, cols, width)
    grad_audio = audio_parts[0]
    for by in (2, 1, 3):
        grad_audio = grad_audio + send(audio_parts[by], turn_x(by))

    square = logits[:cols, 0, :]
    eye = jnp.eye(cols, dtype=bool)
    scores = jnp.sum(jnp.where(eye, square, 0.0), axis=0)
    return (grad_audio, grad_text, row_lse[:cols] - scores, col_lse[0] - scores)


def solution(mesh):
    placed = (P("blk", None), P(("blk", "group"), None))
    return jax.shard_map(
        shards,
        mesh=mesh,
        in_specs=placed,
        out_specs=(
            P(("blk", "group"), None),
            P(("blk", "group"), None),
            P(("blk", "group")),
            P(("blk", "group")),
        ),
        check_vma=False,
    )
```

```python
import jax
import jax.numpy as jnp
from jax import lax
from jax.sharding import PartitionSpec as P

SPAN = 3
BLOCKS = 64
GROUP = 8

logit_scale = 1.0 / 0.07
precise = lax.Precision.HIGHEST
gradient = lax.Precision.HIGH
both = ("blk", "group")


def send(value, target):
    pairs = []
    for block in range(BLOCKS):
        for member in range(GROUP):
            to_block, to_member = target(block, member)
            pairs.append((block * GROUP + member, to_block * GROUP + to_member))
    return lax.ppermute(value, both, pairs)


def ring(by):
    def target(block, member):
        to_block = (block + by) % BLOCKS
        crossed = ((block >> 4) ^ (to_block >> 4)) & 1
        return to_block, member ^ crossed

    return target


def mate(block, member):
    return block ^ 1, member


def across(block, member):
    return block, member ^ 1


def flip_x(bits):
    return lambda block, member: (block, member ^ (bits << 1))


def turn_x(by):
    return lambda block, member: (block, (((member >> 1) + by) % 4) * 2 + (member & 1))


def merge(one, two):
    highest = jnp.maximum(one[0], two[0])
    return jnp.stack(
        [highest, one[1] * jnp.exp(one[0] - highest) + two[1] * jnp.exp(two[0] - highest)]
    )


def rolled(value, by):
    return lax.dynamic_slice_in_dim(jnp.concatenate([value, value], 0), by, 4, 0)


def body(audio_embed, text_embed):
    rows, width = audio_embed.shape
    cols = text_embed.shape[0]
    block = lax.axis_index("blk")
    member = lax.axis_index("group")
    core = block % 2
    x, half = member // 2, member % 2

    two_on = send(text_embed, ring(-2))
    one_on = send(text_embed, ring(-1))
    other_text = send(text_embed, across)

    chunks = audio_embed.reshape(4, 2, cols, width)
    mine = jnp.where(half == 0, chunks[:, 0], chunks[:, 1])
    others = jnp.where(half == 0, chunks[:, 1], chunks[:, 0])
    audio_mine = rolled(mine, x).reshape(4 * cols, width)
    audio = jnp.concatenate([audio_mine, rolled(others, x).reshape(4 * cols, width)])

    def to_plain(value):
        own, other = rolled(value[0:4], (4 - x) % 4), rolled(value[4:8], (4 - x) % 4)
        return jnp.where(half == 0, jnp.stack([own, other], 1), jnp.stack([other, own], 1))

    def from_plain(value):
        own = jnp.where(half == 0, value[:, 0], value[:, 1])
        other = jnp.where(half == 0, value[:, 1], value[:, 0])
        return jnp.concatenate([rolled(own, x), rolled(other, x)])

    window = jnp.stack([text_embed, one_on, two_on])
    logits = logit_scale * jnp.einsum("rd,kcd->rkc", audio, window, precision=precise)
    row_top = jnp.max(logits, axis=(1, 2))
    row_sum = jnp.sum(jnp.exp(logits - row_top[:, None, None]), axis=(1, 2))
    col_top = jnp.max(logits, axis=0)
    col_sum = jnp.sum(jnp.exp(logits - col_top[None]), axis=0)

    row_stat = jnp.stack(
        [to_plain(row_top.reshape(8, cols)), to_plain(row_sum.reshape(8, cols))]
    ).reshape(2, rows)
    col_stat = jnp.stack([col_top, col_sum])
    row_one = send(row_stat, flip_x(1))
    before = send(col_stat, ring(2))
    after = send(col_stat, ring(-2))
    row_stat = merge(row_stat, row_one)
    row_stat = merge(row_stat, send(row_stat, flip_x(3)))
    beside = send(jnp.stack([col_stat, before, after]), mate)
    one_before = jnp.where(core == 0, beside[1], beside[0])
    one_after = jnp.where(core == 0, beside[0], beside[2])
    stat_0 = merge(merge(before[:, 2], one_before[:, 1]), col_stat[:, 0])
    stat_1 = merge(merge(one_before[:, 2], col_stat[:, 1]), one_after[:, 0])
    stat_2 = merge(merge(col_stat[:, 2], one_after[:, 1]), after[:, 0])
    col_stat = jnp.stack([stat_0, stat_1, stat_2], 1)
    col_lse = col_stat[0] + jnp.log(col_stat[1])

    passed = send(jnp.concatenate([row_stat.reshape(-1), col_lse.reshape(-1)]), across)
    other_rows = passed[: 2 * rows].reshape(2, rows)
    other_col_lse = passed[2 * rows :].reshape(SPAN, cols)
    row_stat = merge(row_stat, other_rows)
    row_lse_plain = row_stat[0] + jnp.log(row_stat[1])
    row_lse = from_plain(row_lse_plain.reshape(4, 2, cols)).reshape(rows)

    other_two = send(other_text, ring(-2))
    other_one = send(other_text, ring(-1))
    other_window = jnp.stack([other_text, other_one, other_two])
    other_logits = logit_scale * jnp.einsum(
        "rd,kcd->rkc", audio_mine, other_window, precision=precise
    )

    def weights(scores, by_row, by_col):
        return 0.5 * (
            jnp.exp(scores - by_row[:, None, None]) + jnp.exp(scores - by_col[None])
        )

    shape = (rows, SPAN, cols)
    positive = (lax.broadcasted_iota(jnp.int32, shape, 1) == 0) & (
        lax.broadcasted_iota(jnp.int32, shape, 0) == lax.broadcasted_iota(jnp.int32, shape, 2)
    )
    grad_logits = weights(logits, row_lse, col_lse) - positive.astype(jnp.float32)
    other_grad = weights(other_logits, row_lse[: 4 * cols], other_col_lse)

    text_parts = logit_scale * jnp.einsum("rkc,rd->kcd", grad_logits, audio, precision=gradient)
    from_mate = send(text_parts[1], mate)
    ahead = text_parts[2] + jnp.where(core == 0, from_mate, 0.0)
    grad_text = text_parts[0] + jnp.where(core == 1, from_mate, 0.0) + send(ahead, ring(2))

    audio_parts = logit_scale * (
        jnp.einsum("rkc,kcd->rd", grad_logits[: 4 * cols], window, precision=gradient)
        + jnp.einsum("rkc,kcd->rd", other_grad, other_window, precision=gradient)
    )
    audio_parts = audio_parts.reshape(4, cols, width)
    grad_audio = audio_parts[0]
    for by in (2, 1, 3):
        grad_audio = grad_audio + send(audio_parts[by], turn_x(by))

    square = logits[:cols, 0, :]
    eye = jnp.eye(cols, dtype=bool)
    scores = jnp.sum(jnp.where(eye, square, 0.0), axis=0)
    return (grad_audio, grad_text, row_lse[:cols] - scores, col_lse[0] - scores)


def solution(mesh):
    placed = (P("blk", None), P(("blk", "group"), None))
    return jax.shard_map(
        body,
        mesh=mesh,
        in_specs=placed,
        out_specs=(
            P(("blk", "group"), None),
            P(("blk", "group"), None),
            P(("blk", "group")),
            P(("blk", "group")),
        ),
        check_vma=False,
    )
```
